32 devices in a mesh: seq: 16 (over z, y, core), head: 2 (over x).
Axes of the slice: x: 2, y: 2, z: 4, core: 2. Of those that a mesh axis runs over, the one named last changes fastest.
Arguments:
- tokens: bfloat16 [8192, 5120], P(('seq', 'head')), may hold values from -6 to 6
- w_qkv: bfloat16 [3, 5120, 640], P(None, None, 'head'), may hold values from -0.078125 to 0.078125
- scale_exp: int32 [3, 40, 2], P(None, None, 'head'), may hold values from -2 to 1
- gate_mask: int32 [8192, 2], P('seq', 'head'), may hold values 0 or 1
- rate: float32 [2], P('head'), may hold values from 0.00044194172 to 0.0022097088
- fast_gate: bfloat16 [2, 320, 640], P('head'), may hold values from -0.3125 to 0.3125
- fast_up: bfloat16 [2, 320, 640], P('head'), may hold values from -0.3125 to 0.3125
- fast_down: bfloat16 [2, 320, 640], P('head'), may hold values from -0.25 to 0.25
Outputs:
- answers: bfloat16 [8192, 640], P(('seq', 'head'))
The draws below stay inside these ranges and needn't reach their ends.
All inputs are finite; a program needn't handle non-finite values. No bound on the sum of `gate_mask` on one device may be relied on, other than what follows from the above.
Results may differ from the reference program's by a relative error of at most 0.012.
Values may be sent and summed in bfloat16 or wider, within the bound.
A program may use at most 64 MiB of HBM per device.

```python
import math
import jax
import jax.numpy as jnp
from jax import lax

D = 5120
HD = 320
HID = 640
SB = 128
HEADS = 2
TOKENS = 8192


def plant(drawn, stream_key, least, top_value):
    longest = drawn.shape.index(max(drawn.shape))
    spots = []
    for shift in (0, 1):
        where = [jax.random.randint(jax.random.fold_in(stream_key, axis), (), 0, length) for axis, length in enumerate(drawn.shape)]
        where[longest] = (where[longest] + shift) % drawn.shape[longest]
        spots.append(tuple(where))
    return drawn.at[spots[0]].set(least).at[spots[1]].set(top_value)


def steps_of(rng, shape, shards, smallest, largest):
    loudness, own = 1.0, jax.random.fold_in(rng, 6)
    for axis_at, shards_of in shards:
        steps = jnp.exp(jax.random.uniform(jax.random.fold_in(own, axis_at), (shards_of,), jnp.float32, smallest / len(shards), largest / len(shards)))
        loudness = loudness * jnp.repeat(steps, shape[axis_at] // shards_of).reshape([-1 if axis == axis_at else 1 for axis in range(len(shape))])
    return loudness


def gaussian(key, shape, width, limit, cuts=(), kind=jnp.bfloat16):
    loudness = steps_of(key, shape, cuts, -0.22, 0.18) if cuts else 1.0
    values = jax.random.normal(key, shape, jnp.float32) * width * loudness
    return jnp.minimum(jnp.maximum(values, -limit), limit).astype(kind)


def setup_inputs(seed: int = 0) -> dict:
    streams_of = jax.random.split(jax.random.key(seed), 9)
    tokens = gaussian(streams_of[0], (TOKENS, D), 1.0, 6.0, ((0, 32),))
    w_qkv = gaussian(streams_of[1], (3, D, HEADS * HD), D ** -0.5, 0.078125, ((2, 2),))
    scale_exp = plant(jax.random.randint(streams_of[2], (3, D // SB, HEADS), -2, 2), jax.random.fold_in(streams_of[2], 1), -2, 1).astype(jnp.int32)
    gate_mask = plant((jax.random.randint(streams_of[3], (TOKENS, HEADS), 0, 2) < 1).astype(jnp.int32), jax.random.fold_in(streams_of[3], 1), 0, 1)
    rate = jnp.clip(jnp.exp(math.log(0.0022097088) - 1.609438 * jax.random.uniform(streams_of[4], (HEADS,), jnp.float32) ** steps_of(streams_of[4], (HEADS,), ((0, 2),), -0.2, 0.2)), 0.00044194172, 0.0022097088)
    fast_gate = gaussian(streams_of[5], (HEADS, HD, HID), HD ** -0.5, 0.3125, ((0, 2),))
    fast_up = gaussian(streams_of[6], (HEADS, HD, HID), HD ** -0.5, 0.3125, ((0, 2),))
    fast_down = gaussian(streams_of[7], (HEADS, HD, HID), HID ** -0.5, 0.25, ((0, 2),))
    return dict(tokens=tokens, w_qkv=w_qkv, scale_exp=scale_exp, gate_mask=gate_mask, rate=rate, fast_gate=fast_gate, fast_up=fast_up, fast_down=fast_down)


def expanded(w_qkv, scale_exp):
    factor = jnp.exp2(scale_exp.astype(jnp.float32))
    factor = jnp.repeat(jnp.repeat(factor, SB, axis=1), HD, axis=2)
    return (w_qkv.astype(jnp.float32) * factor).astype(jnp.bfloat16)

def local_grads(keys, values, weight, old):
    gate = jnp.dot(keys, old[0], preferred_element_type=jnp.float32)
    upper = jnp.dot(keys, old[1], preferred_element_type=jnp.float32)
    sigma = jax.nn.sigmoid(gate)
    active = gate * sigma
    hidden = (active * upper).astype(jnp.bfloat16)
    weighted = (weight[:, None] * values.astype(jnp.float32)).astype(jnp.bfloat16)
    d_hidden = jnp.dot(weighted, old[2], preferred_element_type=jnp.float32)
    d_gate = (d_hidden * upper * sigma * (1.0 + gate * (1.0 - sigma))).astype(jnp.bfloat16)
    d_upper = (d_hidden * active).astype(jnp.bfloat16)
    dims = (((0,), (0,)), ((), ()))
    grad_gate = lax.dot_general(keys, d_gate, dims, preferred_element_type=jnp.float32)
    grad_upper = lax.dot_general(keys, d_upper, dims, preferred_element_type=jnp.float32)
    grad_down = lax.dot_general(weighted, hidden, dims, preferred_element_type=jnp.float32)
    return jnp.stack([grad_gate, grad_upper, grad_down])

def respond(query, renorm):
    gate = jnp.dot(query, renorm[0], preferred_element_type=jnp.float32)
    upper = jnp.dot(query, renorm[1], preferred_element_type=jnp.float32)
    hidden = (jax.nn.silu(gate) * upper).astype(jnp.bfloat16)
    output = lax.dot_general(hidden, renorm[2], (((1,), (1,)), ((), ())), preferred_element_type=jnp.float32)
    scaled = output * lax.rsqrt(lax.optimization_barrier(jnp.mean(output * output, axis=-1, keepdims=True)) + 1e-05)
    return scaled.astype(jnp.bfloat16)

def reference(tokens, w_qkv, scale_exp, gate_mask, rate, fast_gate, fast_up, fast_down):
    weff = expanded(w_qkv, scale_exp)
    projected = [jnp.dot(tokens, weff[c], preferred_element_type=jnp.float32).astype(jnp.bfloat16) for c in range(3)]
    split = [p.reshape(TOKENS, HEADS, HD).transpose(1, 0, 2) for p in projected]
    masks = gate_mask.astype(jnp.float32).T

    def one_head(items):
        query, keys, values, mask_row, head_rate, w_gate, w_up, w_down = items
        old = jnp.stack([w_gate, w_up, w_down])
        grads = local_grads(keys, values, head_rate * mask_row, old)
        old_f = old.astype(jnp.float32)
        old_norm = jnp.sqrt(lax.optimization_barrier(jnp.sum(old_f * old_f, axis=1)))
        fresh = old_f + grads
        new_sq = lax.optimization_barrier(jnp.sum(fresh * fresh, axis=1))
        renorm = (fresh * (old_norm / jnp.sqrt(new_sq + 1e-06))[:, None, :]).astype(jnp.bfloat16)
        return respond(query, renorm)
    result = lax.map(one_head, (split[0], split[1], split[2], masks, rate, fast_gate, fast_up, fast_down))
    return result.transpose(1, 0, 2).reshape(TOKENS, HEADS * HD)
```

```python
import functools

import jax
import jax.numpy as jnp
from jax import lax
from jax.experimental import pallas as pl
from jax.experimental.pallas import tpu as pltpu
from jax.sharding import PartitionSpec as P

MESH = pl.DeviceIdType.MESH
F32 = jnp.float32
BF16 = jnp.bfloat16


def dot(a, b, lhs=1, rhs=0):
    return lax.dot_general(a, b, (((lhs,), (rhs,)), ((), ())), preferred_element_type=F32)


def plan(seq, rows):
    factors = (2, seq // 8, 4)
    padded = -(-rows // (16 * seq)) * 16 * seq
    chunks = max(1, min(2, padded // (16 * seq)))
    while (padded // chunks) % (16 * seq):
        chunks -= 1
    return factors, padded, chunks


def kernel(
    sizes,
    tokens_ref, w_hbm, exp_ref, mask_ref, rate_ref, g_ref, u_ref, d_ref,
    out_ref,
    toks, w, acc, grads, buf, tot, recv_c, recv_y, recv_z, renorm, a_send, a_recv,
    tok_sem, w_sem, tsend, trecv, rs_send, rs_recv, ag_send, ag_recv, asend, arecv,
):
    heads, seq, kc, nk, sb, factors, padded, chunks = sizes
    t, hd = tokens_ref.shape[0], w_hbm.shape[2]
    s, me = lax.axis_index("seq"), lax.axis_index("head")
    strides = (1, factors[0], factors[0] * factors[1])
    digits = tuple(lax.rem(lax.div(s, st), f) for st, f in zip(strides, factors))

    def member(phase, step):
        f, st = factors[phase], strides[phase]
        digit = lax.rem(digits[phase] + step, f)
        return digit, (s + (digit - digits[phase]) * st, me)

    def head_peer(step):
        return (s, lax.rem(me + step, heads))

    def tok_copy(k):
        cols = pl.ds(pl.multiple_of(k * kc, kc), kc)
        return pltpu.make_async_copy(tokens_ref.at[:, cols], toks.at[0, :, cols], tok_sem.at[k])

    def w_copy(k):
        rows = pl.ds(pl.multiple_of(k * kc, kc), kc)
        return pltpu.make_async_copy(w_hbm.at[:, rows, :], w.at[:, rows, :], w_sem.at[k])

    def tok_send(step, k):
        cols = pl.ds(pl.multiple_of(k * kc, kc), kc)
        return pltpu.make_async_remote_copy(
            src_ref=tokens_ref.at[:, cols],
            dst_ref=toks.at[heads - step, :, cols],
            send_sem=tsend.at[step - 1, k],
            recv_sem=trecv.at[heads - step - 1, k],
            device_id=head_peer(step),
            device_id_type=MESH,
        )

    def tok_arrival(slot, k):
        cols = pl.ds(pl.multiple_of(k * kc, kc), kc)
        return pltpu.make_async_remote_copy(
            src_ref=tokens_ref.at[:, cols],
            dst_ref=toks.at[slot, :, cols],
            send_sem=tsend.at[slot - 1, k],
            recv_sem=trecv.at[slot - 1, k],
            device_id=head_peer(slot),
            device_id_type=MESH,
        )

    barrier = pltpu.get_barrier_semaphore()
    partners = [head_peer(step) for step in range(1, heads)]
    for phase in range(3):
        partners += [member(phase, step)[1] for step in range(1, factors[phase])]
    for partner in partners:
        pl.semaphore_signal(barrier, inc=1, device_id=partner, device_id_type=MESH)

    def load(k, carry):
        tok_copy(k).start()
        w_copy(k).start()
        return carry

    lax.fori_loop(0, nk, load, 0)
    pl.semaphore_wait(barrier, len(partners))

    def send(k, carry):
        for step in range(1, heads):
            tok_send(step, k).start()
        return carry

    lax.fori_loop(0, nk, send, 0)

    acc[...] = jnp.zeros_like(acc)

    def project(slot, k):
        cols = pl.ds(pl.multiple_of(k * kc, kc), kc)
        x = toks[slot, :, cols]
        for c in range(3):
            acc[c, slot] += dot(x, w[c, cols, :])

    def own(k, carry):
        tok_copy(k).wait()
        w_copy(k).wait()
        for b in range(kc // sb):
            rows = pl.ds(pl.multiple_of(k * kc + b * sb, sb), sb)
            for c in range(3):
                e = exp_ref[c, k * (kc // sb) + b]
                factor = jnp.exp2(jnp.full((1, hd), e, jnp.int32).astype(F32)).astype(BF16)
                w[c, rows, :] = (w[c, rows, :].astype(F32) * factor.astype(F32)).astype(BF16)
        project(0, k)
        return carry

    lax.fori_loop(0, nk, own, 0)
    rate = rate_ref[0]

    def add_grads(slot):
        owner = lax.rem(me + slot, heads)
        mask = mask_ref[pl.ds(pl.multiple_of(owner * t, t), t), :]
        keys = acc[1, slot].astype(BF16)
        values = acc[2, slot].astype(BF16)
        gate = dot(keys, g_ref[0])
        upper = dot(keys, u_ref[0])
        sigma = jax.nn.sigmoid(gate)
        active = gate * sigma
        hidden = (active * upper).astype(BF16)
        weighted = ((rate * mask.astype(F32)) * values.astype(F32)).astype(BF16)
        d_hidden = dot(weighted, d_ref[0])
        d_gate = (d_hidden * upper * sigma * (1.0 + gate * (1.0 - sigma))).astype(BF16)
        d_upper = (d_hidden * active).astype(BF16)
        grads[0] += dot(keys, d_gate, 0, 0)
        grads[1] += dot(keys, d_upper, 0, 0)
        grads[2] += dot(weighted, hidden, 0, 0)

    grads[...] = jnp.zeros_like(grads)
    add_grads(0)

    def others(k, carry):
        for slot in range(1, heads):
            tok_arrival(slot, k).wait_recv()
            project(slot, k)
        return carry

    lax.fori_loop(0, nk, others, 0)

    def other_grads(slot, carry):
        add_grads(slot)
        return carry

    lax.fori_loop(1, heads, other_grads, 0)

    n = hd
    for m in range(3):
        buf[m * n : (m + 1) * n, :] = grads[m].astype(BF16)
    if padded > 3 * n:
        buf[3 * n :, :] = jnp.zeros((padded - 3 * n, buf.shape[1]), BF16)
    span = padded // chunks
    recvs = (recv_c, recv_y, recv_z)

    def region(chunk, phase):
        off, size = chunk * span, span
        for p in range(phase):
            size //= factors[p]
            off = off + digits[p] * size
        return off, size

    def rs_copies(chunk, phase):
        off, size = region(chunk, phase)
        part = size // factors[phase]
        copies = []
        for step in range(1, factors[phase]):
            digit, device = member(phase, step)
            slot = factors[phase] - step - 1
            copies.append(pltpu.make_async_remote_copy(
                src_ref=buf.at[pl.ds(pl.multiple_of(off + digit * part, 16), part), :],
                dst_ref=recvs[phase].at[chunk, slot],
                send_sem=rs_send.at[chunk, phase, step - 1],
                recv_sem=rs_recv.at[chunk, phase, slot],
                device_id=device,
                device_id_type=MESH,
            ))
        return copies

    def rs_finish(chunk, phase, copies):
        for copy in copies:
            copy.wait_recv()
        off, size = region(chunk, phase + 1)
        mine = pl.ds(pl.multiple_of(off, 16), size)
        total = buf[mine, :].astype(F32)
        for slot in range(factors[phase] - 1):
            total = total + recvs[phase][chunk, slot].astype(F32)
        target = tot if phase == 2 else buf
        target[mine, :] = total.astype(BF16)

    def ag_copies(chunk, phase):
        off, size = region(chunk, phase + 1)
        mine = pl.ds(pl.multiple_of(off, 16), size)
        copies = []
        for step in range(1, factors[phase]):
            _, device = member(phase, step)
            copies.append(pltpu.make_async_remote_copy(
                src_ref=tot.at[mine, :],
                dst_ref=tot.at[mine, :],
                send_sem=ag_send.at[chunk, phase, step - 1],
                recv_sem=ag_recv.at[chunk, phase, factors[phase] - step - 1],
                device_id=device,
                device_id_type=MESH,
            ))
        return copies

    def start(copies):
        for copy in copies:
            copy.start()
        return copies

    every = []
    flight = {}
    for tick in range(6 + chunks - 1):
        for chunk in range(chunks):
            stage = tick - chunk
            if stage < 0 or stage > 6:
                continue
            if 1 <= stage <= 3:
                rs_finish(chunk, stage - 1, flight[chunk])
            elif stage > 3:
                for copy in flight[chunk]:
                    copy.wait_recv()
            if stage < 3:
                flight[chunk] = start(rs_copies(chunk, stage))
            elif stage < 6:
                flight[chunk] = start(ag_copies(chunk, 5 - stage))
            every += flight[chunk] if stage < 6 else []
    for chunk in range(chunks):
        stage = 6 + chunks - 1 - chunk
        if stage == 6:
            for copy in flight[chunk]:
                copy.wait_recv()

    for m, ref in enumerate((g_ref, u_ref, d_ref)):
        old = ref[0].astype(F32)
        fresh = old + tot[m * n : (m + 1) * n, :].astype(F32)
        old_norm = jnp.sqrt(jnp.sum(old * old, axis=0, keepdims=True))
        new_norm = jnp.sqrt(jnp.sum(fresh * fresh, axis=0, keepdims=True) + 1e-6)
        renorm[m] = (fresh * (old_norm / new_norm)).astype(BF16)

    def respond(slot):
        query = acc[0, slot].astype(BF16)
        gate = dot(query, renorm[0])
        upper = dot(query, renorm[1])
        hidden = (gate * jax.nn.sigmoid(gate) * upper).astype(BF16)
        output = dot(hidden, renorm[2], 1, 1)
        return (output * lax.rsqrt(jnp.mean(output * output, axis=-1, keepdims=True) + 1e-5)).astype(BF16)

    answers = []
    for step in range(1, heads):
        a_send[step - 1] = respond(step)
        copy = pltpu.make_async_remote_copy(
            src_ref=a_send.at[step - 1],
            dst_ref=a_recv.at[heads - step],
            send_sem=asend.at[step - 1],
            recv_sem=arecv.at[heads - step - 1],
            device_id=head_peer(step),
            device_id_type=MESH,
        )
        copy.start()
        answers.append(copy)
    a_recv[0] = respond(0)
    for copy in answers:
        copy.wait_recv()
    for h in range(heads):
        slot = lax.rem(h - me + heads, heads)
        out_ref[:, h * hd : (h + 1) * hd] = a_recv[slot]

    for copy in answers + every:
        copy.wait_send()

    def sent(k, carry):
        for step in range(1, heads):
            tok_send(step, k).wait_send()
        return carry

    lax.fori_loop(0, nk, sent, 0)


def body(mesh, tokens, w_qkv, scale_exp, gate_mask, rate, fast_gate, fast_up, fast_down):
    heads, seq = mesh.shape["head"], mesh.shape["seq"]
    t, d = tokens.shape
    hd, hid = fast_gate.shape[1:]
    blocks = scale_exp.shape[1]
    sb = d // blocks
    kc = sb * (4 if blocks % 4 == 0 else 1)
    nk = d // kc
    factors, padded, chunks = plan(seq, 3 * hd)
    span = padded // chunks
    parts = []
    size = span
    for f in factors:
        size //= f
        parts.append(size)
    dma = pltpu.SemaphoreType.DMA
    vmem = pl.BlockSpec(memory_space=pltpu.VMEM)
    smem = pl.BlockSpec(memory_space=pltpu.SMEM)
    hbm = pl.BlockSpec(memory_space=pl.ANY)
    most = max(factors) - 1
    return pl.pallas_call(
        functools.partial(kernel, (heads, seq, kc, nk, sb, factors, padded, chunks)),
        out_shape=jax.ShapeDtypeStruct((t, heads * hd), BF16),
        in_specs=[hbm, hbm, smem, vmem, smem, vmem, vmem, vmem],
        out_specs=vmem,
        scratch_shapes=[
            pltpu.VMEM((heads, t, d), BF16),
            pltpu.VMEM((3, d, hd), BF16),
            pltpu.VMEM((3, heads, t, hd), F32),
            pltpu.VMEM((3, hd, hid), F32),
            pltpu.VMEM((padded, hid), BF16),
            pltpu.VMEM((padded, hid), BF16),
            pltpu.VMEM((chunks, factors[0] - 1, parts[0], hid), BF16),
            pltpu.VMEM((chunks, factors[1] - 1, parts[1], hid), BF16),
            pltpu.VMEM((chunks, factors[2] - 1, parts[2], hid), BF16),
            pltpu.VMEM((3, hd, hid), BF16),
            pltpu.VMEM((heads - 1, t, hd), BF16),
            pltpu.VMEM((heads, t, hd), BF16),
            dma((nk,)),
            dma((nk,)),
            dma((heads - 1, nk)),
            dma((heads - 1, nk)),
            dma((chunks, 3, most)),
            dma((chunks, 3, most)),
            dma((chunks, 3, most)),
            dma((chunks, 3, most)),
            dma((heads - 1,)),
            dma((heads - 1,)),
        ],
        compiler_params=pltpu.CompilerParams(
            collective_id=0, has_side_effects=True, vmem_limit_bytes=60 * 1024 * 1024
        ),
    )(
        tokens, w_qkv, scale_exp.reshape(scale_exp.shape[:2]), gate_mask, rate,
        fast_gate, fast_up, fast_down,
    )


def solution(mesh):
    in_specs = (
        P(("seq", "head"), None),
        P(None, None, "head"),
        P(None, None, "head"),
        P("seq", "head"),
        P("head"),
        P("head", None, None),
        P("head", None, None),
        P("head", None, None),
    )
    out_specs = P(("seq", "head"), None)
    return jax.shard_map(
        functools.partial(body, mesh), mesh=mesh, in_specs=in_specs, out_specs=out_specs, check_vma=False
    )
```

```python
import functools

import jax
import jax.numpy as jnp
from jax import lax
from jax.experimental import pallas as pl
from jax.experimental.pallas import tpu as pltpu
from jax.sharding import PartitionSpec as P

MESH = pl.DeviceIdType.MESH
F32 = jnp.float32
BF16 = jnp.bfloat16


def dot(a, b, lhs=1, rhs=0):
    return lax.dot_general(a, b, (((lhs,), (rhs,)), ((), ())), preferred_element_type=F32)


def plan(seq, rows):
    factors = (2, seq // 8, 4)
    padded = -(-rows // (16 * seq)) * 16 * seq
    chunks = max(1, min(2, padded // (16 * seq)))
    while (padded // chunks) % (16 * seq):
        chunks -= 1
    return factors, padded, chunks


def kernel(
    sizes,
    tokens_ref, w_hbm, exp_ref, mask_ref, rate_ref, g_ref, u_ref, d_ref,
    out_ref,
    toks, w, acc, grads, buf, tot, recv_c, recv_y, recv_z, renorm, a_send, a_recv, weights,
    tok_sem, w_sem, tsend, trecv, rs_send, rs_recv, ag_send, ag_recv, asend, arecv,
):
    heads, seq, kc, nk, sb, factors, padded, chunks = sizes
    t, hd = tokens_ref.shape[0], w_hbm.shape[1]
    s, me = lax.axis_index("seq"), lax.axis_index("head")
    strides = (1, factors[0], factors[0] * factors[1])
    digits = tuple(lax.rem(lax.div(s, st), f) for st, f in zip(strides, factors))

    def member(phase, step):
        f, st = factors[phase], strides[phase]
        digit = lax.rem(digits[phase] + step, f)
        return digit, (s + (digit - digits[phase]) * st, me)

    def head_peer(step):
        return (s, lax.rem(me + step, heads))

    def tok_copy(k):
        cols = pl.ds(pl.multiple_of(k * kc, kc), kc)
        return pltpu.make_async_copy(tokens_ref.at[:, cols], toks.at[0, :, cols], tok_sem.at[k])

    def w_copy(k):
        cols = pl.ds(pl.multiple_of(k * kc, kc), kc)
        return pltpu.make_async_copy(w_hbm.at[:, :, cols], w.at[:, :, cols], w_sem.at[k])

    def tok_send(step, k):
        cols = pl.ds(pl.multiple_of(k * kc, kc), kc)
        return pltpu.make_async_remote_copy(
            src_ref=tokens_ref.at[:, cols],
            dst_ref=toks.at[heads - step, :, cols],
            send_sem=tsend.at[step - 1, k],
            recv_sem=trecv.at[heads - step - 1, k],
            device_id=head_peer(step),
            device_id_type=MESH,
        )

    def tok_arrival(slot, k):
        cols = pl.ds(pl.multiple_of(k * kc, kc), kc)
        return pltpu.make_async_remote_copy(
            src_ref=tokens_ref.at[:, cols],
            dst_ref=toks.at[slot, :, cols],
            send_sem=tsend.at[slot - 1, k],
            recv_sem=trecv.at[slot - 1, k],
            device_id=head_peer(slot),
            device_id_type=MESH,
        )

    barrier = pltpu.get_barrier_semaphore()
    partners = [head_peer(step) for step in range(1, heads)]
    for phase in range(3):
        partners += [member(phase, step)[1] for step in range(1, factors[phase])]
    for partner in partners:
        pl.semaphore_signal(barrier, inc=1, device_id=partner, device_id_type=MESH)

    def load(k, carry):
        tok_copy(k).start()
        w_copy(k).start()
        return carry

    lax.fori_loop(0, nk, load, 0)
    pl.semaphore_wait(barrier, len(partners))

    def send(k, carry):
        for step in range(1, heads):
            tok_send(step, k).start()
        return carry

    lax.fori_loop(0, nk, send, 0)

    acc[...] = jnp.zeros_like(acc)

    def project(slot, k):
        cols = pl.ds(pl.multiple_of(k * kc, kc), kc)
        x = toks[slot, :, cols]
        for c in range(3):
            acc[c, slot] += dot(x, w[c, :, cols], 1, 1)

    def own(k, carry):
        tok_copy(k).wait()
        w_copy(k).wait()
        for b in range(kc // sb):
            cols = pl.ds(pl.multiple_of(k * kc + b * sb, sb), sb)
            for c in range(3):
                e = exp_ref[c, 0, k * (kc // sb) + b]
                factor = jnp.exp2(jnp.full((1, sb), e, jnp.int32).astype(F32)).astype(BF16)
                w[c, :, cols] = (w[c, :, cols].astype(F32) * factor.astype(F32)).astype(BF16)
        project(0, k)
        return carry

    lax.fori_loop(0, nk, own, 0)
    weights[...] = jnp.transpose(
        jnp.broadcast_to(rate_ref[0] * mask_ref[...].astype(F32), (128, heads * t))
    )

    def add_grads(slot):
        owner = lax.rem(me + slot, heads)
        weight = weights[pl.ds(pl.multiple_of(owner * t, t), t), :1]
        keys = acc[1, slot].astype(BF16)
        values = acc[2, slot].astype(BF16)
        gate = dot(keys, g_ref[0])
        upper = dot(keys, u_ref[0])
        sigma = jax.nn.sigmoid(gate)
        active = gate * sigma
        hidden = (active * upper).astype(BF16)
        weighted = (weight * values.astype(F32)).astype(BF16)
        d_hidden = dot(weighted, d_ref[0])
        d_gate = (d_hidden * upper * sigma * (1.0 + gate * (1.0 - sigma))).astype(BF16)
        d_upper = (d_hidden * active).astype(BF16)
        grads[0] += dot(keys, d_gate, 0, 0)
        grads[1] += dot(keys, d_upper, 0, 0)
        grads[2] += dot(weighted, hidden, 0, 0)

    grads[...] = jnp.zeros_like(grads)
    add_grads(0)

    def others(k, carry):
        for slot in range(1, heads):
            tok_arrival(slot, k).wait_recv()
            project(slot, k)
        return carry

    lax.fori_loop(0, nk, others, 0)

    def other_grads(slot, carry):
        add_grads(slot)
        return carry

    lax.fori_loop(1, heads, other_grads, 0)

    n = hd
    for m in range(3):
        buf[m * n : (m + 1) * n, :] = grads[m].astype(BF16)
    if padded > 3 * n:
        buf[3 * n :, :] = jnp.zeros((padded - 3 * n, buf.shape[1]), BF16)
    span = padded // chunks
    recvs = (recv_c, recv_y, recv_z)

    def region(chunk, phase):
        off, size = chunk * span, span
        for p in range(phase):
            size //= factors[p]
            off = off + digits[p] * size
        return off, size

    def rs_copies(chunk, phase):
        off, size = region(chunk, phase)
        part = size // factors[phase]
        copies = []
        for step in range(1, factors[phase]):
            digit, device = member(phase, step)
            slot = factors[phase] - step - 1
            copies.append(pltpu.make_async_remote_copy(
                src_ref=buf.at[pl.ds(pl.multiple_of(off + digit * part, 16), part), :],
                dst_ref=recvs[phase].at[chunk, slot],
                send_sem=rs_send.at[chunk, phase, step - 1],
                recv_sem=rs_recv.at[chunk, phase, slot],
                device_id=device,
                device_id_type=MESH,
            ))
        return copies

    def rs_finish(chunk, phase, copies):
        for copy in copies:
            copy.wait_recv()
        off, size = region(chunk, phase + 1)
        mine = pl.ds(pl.multiple_of(off, 16), size)
        total = buf[mine, :].astype(F32)
        for slot in range(factors[phase] - 1):
            total = total + recvs[phase][chunk, slot].astype(F32)
        target = tot if phase == 2 else buf
        target[mine, :] = total.astype(BF16)

    def ag_copies(chunk, phase):
        off, size = region(chunk, phase + 1)
        mine = pl.ds(pl.multiple_of(off, 16), size)
        copies = []
        for step in range(1, factors[phase]):
            _, device = member(phase, step)
            copies.append(pltpu.make_async_remote_copy(
                src_ref=tot.at[mine, :],
                dst_ref=tot.at[mine, :],
                send_sem=ag_send.at[chunk, phase, step - 1],
                recv_sem=ag_recv.at[chunk, phase, factors[phase] - step - 1],
                device_id=device,
                device_id_type=MESH,
            ))
        return copies

    def start(copies):
        for copy in copies:
            copy.start()
        return copies

    every = []
    flight = {}
    for tick in range(6 + chunks - 1):
        for chunk in range(chunks):
            stage = tick - chunk
            if stage < 0 or stage > 6:
                continue
            if 1 <= stage <= 3:
                rs_finish(chunk, stage - 1, flight[chunk])
            elif stage > 3:
                for copy in flight[chunk]:
                    copy.wait_recv()
            if stage < 3:
                flight[chunk] = start(rs_copies(chunk, stage))
            elif stage < 6:
                flight[chunk] = start(ag_copies(chunk, 5 - stage))
            every += flight[chunk] if stage < 6 else []
    for chunk in range(chunks):
        stage = 6 + chunks - 1 - chunk
        if stage == 6:
            for copy in flight[chunk]:
                copy.wait_recv()

    for m, ref in enumerate((g_ref, u_ref, d_ref)):
        old = ref[0].astype(F32)
        fresh = old + tot[m * n : (m + 1) * n, :].astype(F32)
        old_norm = jnp.sqrt(jnp.sum(old * old, axis=0, keepdims=True))
        new_norm = jnp.sqrt(jnp.sum(fresh * fresh, axis=0, keepdims=True) + 1e-6)
        renorm[m] = (fresh * (old_norm / new_norm)).astype(BF16)

    def respond(slot):
        query = acc[0, slot].astype(BF16)
        gate = dot(query, renorm[0])
        upper = dot(query, renorm[1])
        hidden = (gate * jax.nn.sigmoid(gate) * upper).astype(BF16)
        output = dot(hidden, renorm[2], 1, 1)
        return (output * lax.rsqrt(jnp.mean(output * output, axis=-1, keepdims=True) + 1e-5)).astype(BF16)

    answers = []
    for step in range(1, heads):
        a_send[step - 1] = respond(step)
        copy = pltpu.make_async_remote_copy(
            src_ref=a_send.at[step - 1],
            dst_ref=a_recv.at[heads - step],
            send_sem=asend.at[step - 1],
            recv_sem=arecv.at[heads - step - 1],
            device_id=head_peer(step),
            device_id_type=MESH,
        )
        copy.start()
        answers.append(copy)
    a_recv[0] = respond(0)
    for copy in answers:
        copy.wait_recv()
    for h in range(heads):
        slot = lax.rem(h - me + heads, heads)
        out_ref[:, h * hd : (h + 1) * hd] = a_recv[slot]

    for copy in answers + every:
        copy.wait_send()

    def sent(k, carry):
        for step in range(1, heads):
            tok_send(step, k).wait_send()
        return carry

    lax.fori_loop(0, nk, sent, 0)


def body(mesh, tokens, w_qkv, scale_exp, gate_mask, rate, fast_gate, fast_up, fast_down):
    heads, seq = mesh.shape["head"], mesh.shape["seq"]
    t, d = tokens.shape
    hd, hid = fast_gate.shape[1:]
    blocks = scale_exp.shape[1]
    sb = d // blocks
    kc = sb * (4 if blocks % 4 == 0 else 1)
    nk = d // kc
    factors, padded, chunks = plan(seq, 3 * hd)
    span = padded // chunks
    parts = []
    size = span
    for f in factors:
        size //= f
        parts.append(size)
    dma = pltpu.SemaphoreType.DMA
    vmem = pl.BlockSpec(memory_space=pltpu.VMEM)
    smem = pl.BlockSpec(memory_space=pltpu.SMEM)
    hbm = pl.BlockSpec(memory_space=pl.ANY)
    most = max(factors) - 1
    return pl.pallas_call(
        functools.partial(kernel, (heads, seq, kc, nk, sb, factors, padded, chunks)),
        out_shape=jax.ShapeDtypeStruct((t, heads * hd), BF16),
        in_specs=[hbm, hbm, smem, vmem, smem, vmem, vmem, vmem],
        out_specs=vmem,
        scratch_shapes=[
            pltpu.VMEM((heads, t, d), BF16),
            pltpu.VMEM((3, hd, d), BF16),
            pltpu.VMEM((3, heads, t, hd), F32),
            pltpu.VMEM((3, hd, hid), F32),
            pltpu.VMEM((padded, hid), BF16),
            pltpu.VMEM((padded, hid), BF16),
            pltpu.VMEM((chunks, factors[0] - 1, parts[0], hid), BF16),
            pltpu.VMEM((chunks, factors[1] - 1, parts[1], hid), BF16),
            pltpu.VMEM((chunks, factors[2] - 1, parts[2], hid), BF16),
            pltpu.VMEM((3, hd, hid), BF16),
            pltpu.VMEM((heads - 1, t, hd), BF16),
            pltpu.VMEM((heads, t, hd), BF16),
            pltpu.VMEM((heads * t, 128), F32),
            dma((nk,)),
            dma((nk,)),
            dma((heads - 1, nk)),
            dma((heads - 1, nk)),
            dma((chunks, 3, most)),
            dma((chunks, 3, most)),
            dma((chunks, 3, most)),
            dma((chunks, 3, most)),
            dma((heads - 1,)),
            dma((heads - 1,)),
        ],
        compiler_params=pltpu.CompilerParams(
            collective_id=0, has_side_effects=True, vmem_limit_bytes=60 * 1024 * 1024
        ),
    )(
        tokens, w_qkv.swapaxes(1, 2), scale_exp.swapaxes(1, 2), gate_mask.swapaxes(0, 1), rate,
        fast_gate, fast_up, fast_down,
    )


def solution(mesh):
    in_specs = (
        P(("seq", "head"), None),
        P(None, None, "head"),
        P(None, None, "head"),
        P("seq", "head"),
        P("head"),
        P("head", None, None),
        P("head", None, None),
        P("head", None, None),
    )
    out_specs = P(("seq", "head"), None)
    return jax.shard_map(
        functools.partial(body, mesh), mesh=mesh, in_specs=in_specs, out_specs=out_specs, check_vma=False
    )
```

```python
import functools

import jax
import jax.numpy as jnp
from jax import lax
from jax.experimental import pallas as pl
from jax.experimental.pallas import tpu as pltpu
from jax.sharding import PartitionSpec as P

MESH = pl.DeviceIdType.MESH
F32 = jnp.float32
BF16 = jnp.bfloat16


def dot(a, b, lhs=1, rhs=0):
    return lax.dot_general(a, b, (((lhs,), (rhs,)), ((), ())), preferred_element_type=F32)


def plan(seq, rows):
    factors = (2, seq // 8, 4)
    padded = -(-rows // (16 * seq)) * 16 * seq
    chunks = max(1, min(2, padded // (16 * seq)))
    while (padded // chunks) % (16 * seq):
        chunks -= 1
    return factors, padded, chunks


def shared_depth(heads, seq, d, hd, kc):
    unit = 128 * (seq // 2)
    if heads != 2 or hd % 32 or unit % kc:
        return 0
    return (4 * d // 10) // unit * unit


def kernel(
    sizes,
    tokens_ref, w_hbm, exp_ref, mask_ref, rate_ref, g_ref, u_ref, d_ref,
    out_ref,
    toks, w, acc, grads, buf, tot, recv_c, recv_y, recv_z, renorm, a_send, a_recv, weights,
    wsl, wx, pacc, p_send, p_recv,
    tok_sem, w_sem, tsend, trecv, rs_send, rs_recv, ag_send, ag_recv, asend, arecv,
    l_sem, xs, xr, zs, zr, ys, yr, cs, cr, ps, pr,
):
    heads, seq, kc, nk, sb, factors, padded, chunks, depth = sizes
    first = depth // kc
    t, hd = tokens_ref.shape[0], w_hbm.shape[1]
    s, me = lax.axis_index("seq"), lax.axis_index("head")
    strides = (1, factors[0], factors[0] * factors[1])
    digits = tuple(lax.rem(lax.div(s, st), f) for st, f in zip(strides, factors))

    def member(phase, step):
        f, st = factors[phase], strides[phase]
        digit = lax.rem(digits[phase] + step, f)
        return digit, (s + (digit - digits[phase]) * st, me)

    def head_peer(step):
        return (s, lax.rem(me + step, heads))

    def tok_copy(k):
        cols = pl.ds(pl.multiple_of(k * kc, kc), kc)
        return pltpu.make_async_copy(tokens_ref.at[:, cols], toks.at[0, :, cols], tok_sem.at[k])

    def w_copy(k):
        cols = pl.ds(pl.multiple_of(k * kc, kc), kc)
        return pltpu.make_async_copy(w_hbm.at[:, :, cols], w.at[:, :, cols], w_sem.at[k])

    def tok_send(step, k):
        cols = pl.ds(pl.multiple_of(k * kc, kc), kc)
        return pltpu.make_async_remote_copy(
            src_ref=tokens_ref.at[:, cols],
            dst_ref=toks.at[heads - step, :, cols],
            send_sem=tsend.at[step - 1, k],
            recv_sem=trecv.at[heads - step - 1, k],
            device_id=head_peer(step),
            device_id_type=MESH,
        )

    def tok_arrival(slot, k):
        cols = pl.ds(pl.multiple_of(k * kc, kc), kc)
        return pltpu.make_async_remote_copy(
            src_ref=tokens_ref.at[:, cols],
            dst_ref=toks.at[slot, :, cols],
            send_sem=tsend.at[slot - 1, k],
            recv_sem=trecv.at[slot - 1, k],
            device_id=head_peer(slot),
            device_id_type=MESH,
        )

    barrier = pltpu.get_barrier_semaphore()
    partners = [head_peer(step) for step in range(1, heads)]
    for phase in range(3):
        partners += [member(phase, step)[1] for step in range(1, factors[phase])]
    for partner in partners:
        pl.semaphore_signal(barrier, inc=1, device_id=partner, device_id_type=MESH)

    def load(k, carry):
        tok_copy(k).start()
        w_copy(k).start()
        return carry

    every = []

    def start(copies):
        for copy in copies:
            copy.start()
        every.extend(copies)
        return copies

    core, y, z = digits
    half, width = hd // 2, wsl.shape[2]
    chip = y + factors[1] * z

    def piece(m, zrel, yrel, c):
        at = lax.rem(y + yrel, factors[1]) + factors[1] * lax.rem(z + zrel, factors[2])
        return wx.at[
            m,
            pl.ds(pl.multiple_of(c * half, 16), half),
            pl.ds(pl.multiple_of(at * width, 128), width),
        ]

    def remote(src, dst, send_sem, recv_sem, device):
        return pltpu.make_async_remote_copy(
            src_ref=src, dst_ref=dst, send_sem=send_sem, recv_sem=recv_sem,
            device_id=device, device_id_type=MESH,
        )

    def over_x(m):
        return remote(wsl.at[m], piece(m, 0, 0, core), xs.at[m], xr.at[m], head_peer(1))

    def along_z(m, step):
        own_piece = piece(m, 0, 0, core)
        return remote(own_piece, own_piece, zs.at[m, step - 1], zr.at[m, factors[2] - step - 1], member(2, step)[1])

    def z_arrival(m, slot):
        where = piece(m, slot + 1, 0, core)
        return remote(where, where, zs.at[m, slot], zr.at[m, slot], member(2, 1)[1])

    def over_y(m, zrel, step):
        where = piece(m, zrel, 0, core)
        return remote(where, where, ys.at[m, zrel, step - 1], yr.at[m, zrel, factors[1] - step - 1], member(1, step)[1])

    def y_arrival(m, zrel, slot):
        where = piece(m, zrel, slot + 1, core)
        return remote(where, where, ys.at[m, zrel, slot], yr.at[m, zrel, slot], member(1, 1)[1])

    def to_core(m, zrel, yrel):
        where = piece(m, zrel, yrel, core)
        return remote(where, where, cs.at[m, zrel, yrel], cr.at[m, zrel, yrel], member(0, 1)[1])

    def core_arrival(m, zrel, yrel):
        where = piece(m, zrel, yrel, 1 - core)
        return remote(where, where, cs.at[m, zrel, yrel], cr.at[m, zrel, yrel], member(0, 1)[1])

    def forward(m, zrel):
        start([over_y(m, zrel, step) for step in range(1, factors[1])] + [to_core(m, zrel, 0)])

    def take_x(m):
        over_x(m).wait_recv()
        start([along_z(m, step) for step in range(1, factors[2])])
        forward(m, 0)

    def take_z(m):
        for slot in range(factors[2] - 1):
            z_arrival(m, slot).wait_recv()
            forward(m, slot + 1)

    def take_y(m):
        for zrel in range(factors[2]):
            for slot in range(factors[1] - 1):
                y_arrival(m, zrel, slot).wait_recv()
                start([to_core(m, zrel, slot + 1)])

    def partial_copy(m):
        return remote(p_send.at[m], p_recv.at[m], ps.at[m], pr.at[m], head_peer(1))

    def answer_partial(m):
        for zrel in range(factors[2]):
            for yrel in range(factors[1]):
                core_arrival(m, zrel, yrel).wait_recv()
        pacc[...] = jnp.zeros_like(pacc)

        def add(k, carry):
            cols = pl.ds(pl.multiple_of(k * kc, kc), kc)
            pacc[...] += dot(toks[0, :, cols], wx[m, :, cols], 1, 1)
            return carry

        lax.fori_loop(0, first, add, 0)
        p_send[m] = pacc[...].astype(BF16)
        start([partial_copy(m)])

    def take_partial(m):
        partial_copy(m).wait_recv()
        acc[m, 1] += p_recv[m].astype(F32)

    def factor_of(c, block):
        e = jnp.full((1, sb), exp_ref[c, 0, block], jnp.int32).astype(F32)
        return jnp.exp2(e).astype(BF16).astype(F32)

    if depth:
        w_slice = pltpu.make_async_copy(
            w_hbm.at[
                :,
                pl.ds(pl.multiple_of(core * half, 16), half),
                pl.ds(pl.multiple_of(chip * width, 128), width),
            ],
            wsl, l_sem.at[0],
        )
        w_slice.start()
    lax.fori_loop(0, nk, load, 0)
    if depth:
        w_slice.wait()
        for c in range(3):
            for b in range(width // sb):
                cols = pl.ds(b * sb, sb)
                scale = factor_of(c, chip * (width // sb) + b)
                wsl[c, :, cols] = (wsl[c, :, cols].astype(F32) * scale).astype(BF16)
    pl.semaphore_wait(barrier, len(partners))
    if depth:
        start([over_x(m) for m in (1, 2, 0)])
        for m in (1, 2, 0):
            take_x(m)

    def send(k, carry):
        for step in range(1, heads):
            tok_send(step, k).start()
        return carry

    lax.fori_loop(first, nk, send, 0)

    acc[...] = jnp.zeros_like(acc)

    def project(slot, k):
        cols = pl.ds(pl.multiple_of(k * kc, kc), kc)
        x = toks[slot, :, cols]
        for c in range(3):
            acc[c, slot] += dot(x, w[c, :, cols], 1, 1)

    def own(k, carry):
        tok_copy(k).wait()
        w_copy(k).wait()
        for b in range(kc // sb):
            cols = pl.ds(pl.multiple_of(k * kc + b * sb, sb), sb)
            for c in range(3):
                scale = factor_of(c, k * (kc // sb) + b)
                w[c, :, cols] = (w[c, :, cols].astype(F32) * scale).astype(BF16)
        project(0, k)
        return carry

    lax.fori_loop(0, nk, own, 0)
    weights[...] = jnp.transpose(
        jnp.broadcast_to(rate_ref[0] * mask_ref[...].astype(F32), (128, heads * t))
    )

    def add_grads(slot):
        owner = lax.rem(me + slot, heads)
        weight = weights[pl.ds(pl.multiple_of(owner * t, t), t), :1]
        keys = acc[1, slot].astype(BF16)
        values = acc[2, slot].astype(BF16)
        gate = dot(keys, g_ref[0])
        upper = dot(keys, u_ref[0])
        sigma = jax.nn.sigmoid(gate)
        active = gate * sigma
        hidden = (active * upper).astype(BF16)
        weighted = (weight * values.astype(F32)).astype(BF16)
        d_hidden = dot(weighted, d_ref[0])
        d_gate = (d_hidden * upper * sigma * (1.0 + gate * (1.0 - sigma))).astype(BF16)
        d_upper = (d_hidden * active).astype(BF16)
        grads[0] += dot(keys, d_gate, 0, 0)
        grads[1] += dot(keys, d_upper, 0, 0)
        grads[2] += dot(weighted, hidden, 0, 0)

    grads[...] = jnp.zeros_like(grads)
    add_grads(0)

    if depth:
        take_z(1)
        take_z(2)
        take_y(1)
        answer_partial(1)
        take_y(2)
        answer_partial(2)
        take_z(0)

    def others(k, carry):
        for slot in range(1, heads):
            tok_arrival(slot, k).wait_recv()
            project(slot, k)
        return carry

    lax.fori_loop(first, nk, others, 0)
    if depth:
        take_partial(1)
        take_partial(2)

    def other_grads(slot, carry):
        add_grads(slot)
        return carry

    lax.fori_loop(1, heads, other_grads, 0)

    n = hd
    for m in range(3):
        buf[m * n : (m + 1) * n, :] = grads[m].astype(BF16)
    if padded > 3 * n:
        buf[3 * n :, :] = jnp.zeros((padded - 3 * n, buf.shape[1]), BF16)
    span = padded // chunks
    recvs = (recv_c, recv_y, recv_z)

    def region(chunk, phase):
        off, size = chunk * span, span
        for p in range(phase):
            size //= factors[p]
            off = off + digits[p] * size
        return off, size

    def rs_copies(chunk, phase):
        off, size = region(chunk, phase)
        part = size // factors[phase]
        copies = []
        for step in range(1, factors[phase]):
            digit, device = member(phase, step)
            slot = factors[phase] - step - 1
            copies.append(pltpu.make_async_remote_copy(
                src_ref=buf.at[pl.ds(pl.multiple_of(off + digit * part, 16), part), :],
                dst_ref=recvs[phase].at[chunk, slot],
                send_sem=rs_send.at[chunk, phase, step - 1],
                recv_sem=rs_recv.at[chunk, phase, slot],
                device_id=device,
                device_id_type=MESH,
            ))
        return copies

    def rs_finish(chunk, phase, copies):
        for copy in copies:
            copy.wait_recv()
        off, size = region(chunk, phase + 1)
        mine = pl.ds(pl.multiple_of(off, 16), size)
        total = buf[mine, :].astype(F32)
        for slot in range(factors[phase] - 1):
            total = total + recvs[phase][chunk, slot].astype(F32)
        target = tot if phase == 2 else buf
        target[mine, :] = total.astype(BF16)

    def ag_copies(chunk, phase):
        off, size = region(chunk, phase + 1)
        mine = pl.ds(pl.multiple_of(off, 16), size)
        copies = []
        for step in range(1, factors[phase]):
            _, device = member(phase, step)
            copies.append(pltpu.make_async_remote_copy(
                src_ref=tot.at[mine, :],
                dst_ref=tot.at[mine, :],
                send_sem=ag_send.at[chunk, phase, step - 1],
                recv_sem=ag_recv.at[chunk, phase, factors[phase] - step - 1],
                device_id=device,
                device_id_type=MESH,
            ))
        return copies

    flight = {}
    for tick in range(6 + chunks - 1):
        for chunk in range(chunks):
            stage = tick - chunk
            if stage < 0 or stage > 6:
                continue
            if 1 <= stage <= 3:
                rs_finish(chunk, stage - 1, flight[chunk])
            elif stage > 3:
                for copy in flight[chunk]:
                    copy.wait_recv()
            if stage < 3:
                flight[chunk] = start(rs_copies(chunk, stage))
            elif stage < 6:
                flight[chunk] = start(ag_copies(chunk, 5 - stage))
        if depth and tick == 2:
            take_y(0)
            answer_partial(0)
    for chunk in range(chunks):
        stage = 6 + chunks - 1 - chunk
        if stage == 6:
            for copy in flight[chunk]:
                copy.wait_recv()

    for m, ref in enumerate((g_ref, u_ref, d_ref)):
        old = ref[0].astype(F32)
        fresh = old + tot[m * n : (m + 1) * n, :].astype(F32)
        old_norm = jnp.sqrt(jnp.sum(old * old, axis=0, keepdims=True))
        new_norm = jnp.sqrt(jnp.sum(fresh * fresh, axis=0, keepdims=True) + 1e-6)
        renorm[m] = (fresh * (old_norm / new_norm)).astype(BF16)

    def respond(slot):
        query = acc[0, slot].astype(BF16)
        gate = dot(query, renorm[0])
        upper = dot(query, renorm[1])
        hidden = (gate * jax.nn.sigmoid(gate) * upper).astype(BF16)
        output = dot(hidden, renorm[2], 1, 1)
        return (output * lax.rsqrt(jnp.mean(output * output, axis=-1, keepdims=True) + 1e-5)).astype(BF16)

    if depth:
        take_partial(0)
    answers = []
    for step in range(1, heads):
        a_send[step - 1] = respond(step)
        copy = pltpu.make_async_remote_copy(
            src_ref=a_send.at[step - 1],
            dst_ref=a_recv.at[heads - step],
            send_sem=asend.at[step - 1],
            recv_sem=arecv.at[heads - step - 1],
            device_id=head_peer(step),
            device_id_type=MESH,
        )
        copy.start()
        answers.append(copy)
    a_recv[0] = respond(0)
    for copy in answers:
        copy.wait_recv()
    for h in range(heads):
        slot = lax.rem(h - me + heads, heads)
        out_ref[:, h * hd : (h + 1) * hd] = a_recv[slot]

    for copy in answers + every:
        copy.wait_send()

    def sent(k, carry):
        for step in range(1, heads):
            tok_send(step, k).wait_send()
        return carry

    lax.fori_loop(first, nk, sent, 0)


def body(mesh, tokens, w_qkv, scale_exp, gate_mask, rate, fast_gate, fast_up, fast_down):
    heads, seq = mesh.shape["head"], mesh.shape["seq"]
    t, d = tokens.shape
    hd, hid = fast_gate.shape[1:]
    blocks = scale_exp.shape[1]
    sb = d // blocks
    kc = sb * (4 if blocks % 4 == 0 else 1)
    nk = d // kc
    factors, padded, chunks = plan(seq, 3 * hd)
    span = padded // chunks
    parts = []
    size = span
    for f in factors:
        size //= f
        parts.append(size)
    dma = pltpu.SemaphoreType.DMA
    vmem = pl.BlockSpec(memory_space=pltpu.VMEM)
    smem = pl.BlockSpec(memory_space=pltpu.SMEM)
    hbm = pl.BlockSpec(memory_space=pl.ANY)
    most = max(factors) - 1
    depth = shared_depth(heads, seq, d, hd, kc)
    width = max(depth // (seq // 2), 128)
    f1, f2 = factors[1:]
    return pl.pallas_call(
        functools.partial(kernel, (heads, seq, kc, nk, sb, factors, padded, chunks, depth)),
        out_shape=jax.ShapeDtypeStruct((t, heads * hd), BF16),
        in_specs=[hbm, hbm, smem, vmem, smem, vmem, vmem, vmem],
        out_specs=vmem,
        scratch_shapes=[
            pltpu.VMEM((heads, t, d), BF16),
            pltpu.VMEM((3, hd, d), BF16),
            pltpu.VMEM((3, heads, t, hd), F32),
            pltpu.VMEM((3, hd, hid), F32),
            pltpu.VMEM((padded, hid), BF16),
            pltpu.VMEM((padded, hid), BF16),
            pltpu.VMEM((chunks, factors[0] - 1, parts[0], hid), BF16),
            pltpu.VMEM((chunks, factors[1] - 1, parts[1], hid), BF16),
            pltpu.VMEM((chunks, factors[2] - 1, parts[2], hid), BF16),
            pltpu.VMEM((3, hd, hid), BF16),
            pltpu.VMEM((heads - 1, t, hd), BF16),
            pltpu.VMEM((heads, t, hd), BF16),
            pltpu.VMEM((heads * t, 128), F32),
            pltpu.VMEM((3, hd // 2, width), BF16),
            pltpu.VMEM((3, hd, max(depth, 128)), BF16),
            pltpu.VMEM((t, hd), F32),
            pltpu.VMEM((3, t, hd), BF16),
            pltpu.VMEM((3, t, hd), BF16),
            dma((nk,)),
            dma((nk,)),
            dma((heads - 1, nk)),
            dma((heads - 1, nk)),
            dma((chunks, 3, most)),
            dma((chunks, 3, most)),
            dma((chunks, 3, most)),
            dma((chunks, 3, most)),
            dma((heads - 1,)),
            dma((heads - 1,)),
            dma((1,)),
            dma((3,)),
            dma((3,)),
            dma((3, f2 - 1)),
            dma((3, f2 - 1)),
            dma((3, f2, f1 - 1)),
            dma((3, f2, f1 - 1)),
            dma((3, f2, f1)),
            dma((3, f2, f1)),
            dma((3,)),
            dma((3,)),
        ],
        compiler_params=pltpu.CompilerParams(
            collective_id=0, has_side_effects=True, vmem_limit_bytes=60 * 1024 * 1024
        ),
    )(
        tokens, w_qkv.swapaxes(1, 2), scale_exp.swapaxes(1, 2), gate_mask.swapaxes(0, 1), rate,
        fast_gate, fast_up, fast_down,
    )


def solution(mesh):
    in_specs = (
        P(("seq", "head"), None),
        P(None, None, "head"),
        P(None, None, "head"),
        P("seq", "head"),
        P("head"),
        P("head", None, None),
        P("head", None, None),
        P("head", None, None),
    )
    out_specs = P(("seq", "head"), None)
    return jax.shard_map(
        functools.partial(body, mesh), mesh=mesh, in_specs=in_specs, out_specs=out_specs, check_vma=False
    )
```

```python
import functools

import jax
import jax.numpy as jnp
from jax import lax
from jax.experimental import pallas as pl
from jax.experimental.pallas import tpu as pltpu
from jax.sharding import PartitionSpec as P

MESH = pl.DeviceIdType.MESH
F32 = jnp.float32
BF16 = jnp.bfloat16


def dot(a, b, lhs=1, rhs=0):
    return lax.dot_general(a, b, (((lhs,), (rhs,)), ((), ())), preferred_element_type=F32)


def plan(seq, rows):
    factors = (2, seq // 8, 4)
    padded = -(-rows // (16 * seq)) * 16 * seq
    chunks = max(1, min(2, padded // (16 * seq)))
    while (padded // chunks) % (16 * seq):
        chunks -= 1
    return factors, padded, chunks


def shared_depth(heads, seq, d, hd, kc):
    unit = 128 * (seq // 2)
    if heads != 2 or hd % 32 or unit % kc:
        return 0
    return (6 * d // 10) // unit * unit


def kernel(
    sizes,
    tokens_ref, w_hbm, exp_ref, mask_ref, rate_ref, g_ref, u_ref, d_ref,
    out_ref,
    toks, w, acc, grads, buf, tot, recv_c, recv_y, recv_z, renorm, a_send, a_recv, weights,
    wsl, wx, pacc, p_send, p_recv,
    tok_sem, w_sem, tsend, trecv, rs_send, rs_recv, ag_send, ag_recv, asend, arecv,
    l_sem, xs, xr, zs, zr, ys, yr, cs, cr, ps, pr,
):
    heads, seq, kc, nk, sb, factors, padded, chunks, depth = sizes
    first = depth // kc
    t, hd = tokens_ref.shape[0], w_hbm.shape[1]
    s, me = lax.axis_index("seq"), lax.axis_index("head")
    strides = (1, factors[0], factors[0] * factors[1])
    digits = tuple(lax.rem(lax.div(s, st), f) for st, f in zip(strides, factors))

    def member(phase, step):
        f, st = factors[phase], strides[phase]
        digit = lax.rem(digits[phase] + step, f)
        return digit, (s + (digit - digits[phase]) * st, me)

    def head_peer(step):
        return (s, lax.rem(me + step, heads))

    def tok_copy(k):
        cols = pl.ds(pl.multiple_of(k * kc, kc), kc)
        return pltpu.make_async_copy(tokens_ref.at[:, cols], toks.at[0, :, cols], tok_sem.at[k])

    def w_copy(k):
        cols = pl.ds(pl.multiple_of(k * kc, kc), kc)
        return pltpu.make_async_copy(w_hbm.at[:, :, cols], w.at[:, :, cols], w_sem.at[k])

    def tok_send(step, k):
        cols = pl.ds(pl.multiple_of(k * kc, kc), kc)
        return pltpu.make_async_remote_copy(
            src_ref=tokens_ref.at[:, cols],
            dst_ref=toks.at[heads - step, :, cols],
            send_sem=tsend.at[step - 1, k],
            recv_sem=trecv.at[heads - step - 1, k],
            device_id=head_peer(step),
            device_id_type=MESH,
        )

    def tok_arrival(slot, k):
        cols = pl.ds(pl.multiple_of(k * kc, kc), kc)
        return pltpu.make_async_remote_copy(
            src_ref=tokens_ref.at[:, cols],
            dst_ref=toks.at[slot, :, cols],
            send_sem=tsend.at[slot - 1, k],
            recv_sem=trecv.at[slot - 1, k],
            device_id=head_peer(slot),
            device_id_type=MESH,
        )

    barrier = pltpu.get_barrier_semaphore()
    partners = [head_peer(step) for step in range(1, heads)]
    for phase in range(3):
        partners += [member(phase, step)[1] for step in range(1, factors[phase])]
    for partner in partners:
        pl.semaphore_signal(barrier, inc=1, device_id=partner, device_id_type=MESH)

    def load(k, carry):
        tok_copy(k).start()
        w_copy(k).start()
        return carry

    every = []

    def start(copies):
        for copy in copies:
            copy.start()
        every.extend(copies)
        return copies

    core, y, z = digits
    half, width = hd // 2, wsl.shape[2]
    chip = y + factors[1] * z

    def piece(m, zrel, yrel, c):
        at = lax.rem(y + yrel, factors[1]) + factors[1] * lax.rem(z + zrel, factors[2])
        return wx.at[
            m,
            pl.ds(pl.multiple_of(c * half, 16), half),
            pl.ds(pl.multiple_of(at * width, 128), width),
        ]

    def remote(src, dst, send_sem, recv_sem, device):
        return pltpu.make_async_remote_copy(
            src_ref=src, dst_ref=dst, send_sem=send_sem, recv_sem=recv_sem,
            device_id=device, device_id_type=MESH,
        )

    def over_x(m):
        return remote(wsl.at[m], piece(m, 0, 0, core), xs.at[m], xr.at[m], head_peer(1))

    def along_z(m, step):
        own_piece = piece(m, 0, 0, core)
        return remote(own_piece, own_piece, zs.at[m, step - 1], zr.at[m, factors[2] - step - 1], member(2, step)[1])

    def z_arrival(m, slot):
        where = piece(m, slot + 1, 0, core)
        return remote(where, where, zs.at[m, slot], zr.at[m, slot], member(2, 1)[1])

    def over_y(m, zrel, step):
        where = piece(m, zrel, 0, core)
        return remote(where, where, ys.at[m, zrel, step - 1], yr.at[m, zrel, factors[1] - step - 1], member(1, step)[1])

    def y_arrival(m, zrel, slot):
        where = piece(m, zrel, slot + 1, core)
        return remote(where, where, ys.at[m, zrel, slot], yr.at[m, zrel, slot], member(1, 1)[1])

    def to_core(m, zrel, yrel):
        where = piece(m, zrel, yrel, core)
        return remote(where, where, cs.at[m, zrel, yrel], cr.at[m, zrel, yrel], member(0, 1)[1])

    def core_arrival(m, zrel, yrel):
        where = piece(m, zrel, yrel, 1 - core)
        return remote(where, where, cs.at[m, zrel, yrel], cr.at[m, zrel, yrel], member(0, 1)[1])

    def forward(m, zrel):
        start([over_y(m, zrel, step) for step in range(1, factors[1])] + [to_core(m, zrel, 0)])

    def take_x(m):
        over_x(m).wait_recv()
        start([along_z(m, step) for step in range(1, factors[2])])
        forward(m, 0)

    def take_z(m):
        for slot in range(factors[2] - 1):
            z_arrival(m, slot).wait_recv()
            forward(m, slot + 1)

    def take_y(m):
        for zrel in range(factors[2]):
            for slot in range(factors[1] - 1):
                y_arrival(m, zrel, slot).wait_recv()
                start([to_core(m, zrel, slot + 1)])

    def partial_copy(m):
        return remote(p_send.at[m], p_recv.at[m], ps.at[m], pr.at[m], head_peer(1))

    def answer_partial(m):
        for zrel in range(factors[2]):
            for yrel in range(factors[1]):
                core_arrival(m, zrel, yrel).wait_recv()
        pacc[...] = jnp.zeros_like(pacc)

        def add(k, carry):
            cols = pl.ds(pl.multiple_of(k * kc, kc), kc)
            pacc[...] += dot(toks[0, :, cols], wx[m, :, cols], 1, 1)
            return carry

        lax.fori_loop(0, first, add, 0)
        p_send[m] = pacc[...].astype(BF16)
        start([partial_copy(m)])

    def take_partial(m):
        partial_copy(m).wait_recv()
        acc[m, 1] += p_recv[m].astype(F32)

    def factor_of(c, block):
        e = jnp.full((1, sb), exp_ref[c, 0, block], jnp.int32).astype(F32)
        return jnp.exp2(e).astype(BF16).astype(F32)

    if depth:
        w_slice = pltpu.make_async_copy(
            w_hbm.at[
                :,
                pl.ds(pl.multiple_of(core * half, 16), half),
                pl.ds(pl.multiple_of(chip * width, 128), width),
            ],
            wsl, l_sem.at[0],
        )
        w_slice.start()
    lax.fori_loop(0, nk, load, 0)
    if depth:
        w_slice.wait()
        for c in range(3):
            for b in range(width // sb):
                cols = pl.ds(b * sb, sb)
                scale = factor_of(c, chip * (width // sb) + b)
                wsl[c, :, cols] = (wsl[c, :, cols].astype(F32) * scale).astype(BF16)
    pl.semaphore_wait(barrier, len(partners))
    if depth:
        start([over_x(m) for m in (1, 2, 0)])
        for m in (1, 2, 0):
            take_x(m)

    def send(k, carry):
        for step in range(1, heads):
            tok_send(step, k).start()
        return carry

    lax.fori_loop(first, nk, send, 0)

    acc[...] = jnp.zeros_like(acc)

    def project(slot, k):
        cols = pl.ds(pl.multiple_of(k * kc, kc), kc)
        x = toks[slot, :, cols]
        for c in range(3):
            acc[c, slot] += dot(x, w[c, :, cols], 1, 1)

    def own(k, carry):
        tok_copy(k).wait()
        w_copy(k).wait()
        for b in range(kc // sb):
            cols = pl.ds(pl.multiple_of(k * kc + b * sb, sb), sb)
            for c in range(3):
                scale = factor_of(c, k * (kc // sb) + b)
                w[c, :, cols] = (w[c, :, cols].astype(F32) * scale).astype(BF16)
        project(0, k)
        return carry

    lax.fori_loop(0, nk, own, 0)
    if depth:
        take_z(1)
    weights[...] = jnp.transpose(
        jnp.broadcast_to(rate_ref[0] * mask_ref[...].astype(F32), (128, heads * t))
    )

    def add_grads(slot):
        owner = lax.rem(me + slot, heads)
        weight = weights[pl.ds(pl.multiple_of(owner * t, t), t), :1]
        keys = acc[1, slot].astype(BF16)
        values = acc[2, slot].astype(BF16)
        gate = dot(keys, g_ref[0])
        upper = dot(keys, u_ref[0])
        sigma = jax.nn.sigmoid(gate)
        active = gate * sigma
        hidden = (active * upper).astype(BF16)
        weighted = (weight * values.astype(F32)).astype(BF16)
        d_hidden = dot(weighted, d_ref[0])
        d_gate = (d_hidden * upper * sigma * (1.0 + gate * (1.0 - sigma))).astype(BF16)
        d_upper = (d_hidden * active).astype(BF16)
        grads[0] += dot(keys, d_gate, 0, 0)
        grads[1] += dot(keys, d_upper, 0, 0)
        grads[2] += dot(weighted, hidden, 0, 0)

    if depth:
        take_z(2)
    grads[...] = jnp.zeros_like(grads)
    add_grads(0)

    if depth:
        take_y(1)
        answer_partial(1)
        take_y(2)
        answer_partial(2)
        take_z(0)

    def others(k, carry):
        for slot in range(1, heads):
            tok_arrival(slot, k).wait_recv()
            project(slot, k)
        return carry

    lax.fori_loop(first, nk, others, 0)
    if depth:
        take_partial(1)
        take_partial(2)

    def other_grads(slot, carry):
        add_grads(slot)
        return carry

    lax.fori_loop(1, heads, other_grads, 0)

    n = hd
    for m in range(3):
        buf[m * n : (m + 1) * n, :] = grads[m].astype(BF16)
    if padded > 3 * n:
        buf[3 * n :, :] = jnp.zeros((padded - 3 * n, buf.shape[1]), BF16)
    span = padded // chunks
    recvs = (recv_c, recv_y, recv_z)

    def region(chunk, phase):
        off, size = chunk * span, span
        for p in range(phase):
            size //= factors[p]
            off = off + digits[p] * size
        return off, size

    def rs_copies(chunk, phase):
        off, size = region(chunk, phase)
        part = size // factors[phase]
        copies = []
        for step in range(1, factors[phase]):
            digit, device = member(phase, step)
            slot = factors[phase] - step - 1
            copies.append(pltpu.make_async_remote_copy(
                src_ref=buf.at[pl.ds(pl.multiple_of(off + digit * part, 16), part), :],
                dst_ref=recvs[phase].at[chunk, slot],
                send_sem=rs_send.at[chunk, phase, step - 1],
                recv_sem=rs_recv.at[chunk, phase, slot],
                device_id=device,
                device_id_type=MESH,
            ))
        return copies

    def rs_finish(chunk, phase, copies):
        for copy in copies:
            copy.wait_recv()
        off, size = region(chunk, phase + 1)
        mine = pl.ds(pl.multiple_of(off, 16), size)
        total = buf[mine, :].astype(F32)
        for slot in range(factors[phase] - 1):
            total = total + recvs[phase][chunk, slot].astype(F32)
        target = tot if phase == 2 else buf
        target[mine, :] = total.astype(BF16)

    def ag_copies(chunk, phase):
        off, size = region(chunk, phase + 1)
        mine = pl.ds(pl.multiple_of(off, 16), size)
        copies = []
        for step in range(1, factors[phase]):
            _, device = member(phase, step)
            copies.append(pltpu.make_async_remote_copy(
                src_ref=tot.at[mine, :],
                dst_ref=tot.at[mine, :],
                send_sem=ag_send.at[chunk, phase, step - 1],
                recv_sem=ag_recv.at[chunk, phase, factors[phase] - step - 1],
                device_id=device,
                device_id_type=MESH,
            ))
        return copies

    flight = {}
    for tick in range(6 + chunks - 1):
        for chunk in range(chunks):
            stage = tick - chunk
            if stage < 0 or stage > 6:
                continue
            if 1 <= stage <= 3:
                rs_finish(chunk, stage - 1, flight[chunk])
            elif stage > 3:
                for copy in flight[chunk]:
                    copy.wait_recv()
            if stage < 3:
                flight[chunk] = start(rs_copies(chunk, stage))
            elif stage < 6:
                flight[chunk] = start(ag_copies(chunk, 5 - stage))
        if depth and tick == 4:
            take_y(0)
            answer_partial(0)
    for chunk in range(chunks):
        stage = 6 + chunks - 1 - chunk
        if stage == 6:
            for copy in flight[chunk]:
                copy.wait_recv()

    for m, ref in enumerate((g_ref, u_ref, d_ref)):
        old = ref[0].astype(F32)
        fresh = old + tot[m * n : (m + 1) * n, :].astype(F32)
        old_norm = jnp.sqrt(jnp.sum(old * old, axis=0, keepdims=True))
        new_norm = jnp.sqrt(jnp.sum(fresh * fresh, axis=0, keepdims=True) + 1e-6)
        renorm[m] = (fresh * (old_norm / new_norm)).astype(BF16)

    def respond(slot):
        query = acc[0, slot].astype(BF16)
        gate = dot(query, renorm[0])
        upper = dot(query, renorm[1])
        hidden = (gate * jax.nn.sigmoid(gate) * upper).astype(BF16)
        output = dot(hidden, renorm[2], 1, 1)
        return (output * lax.rsqrt(jnp.mean(output * output, axis=-1, keepdims=True) + 1e-5)).astype(BF16)

    if depth:
        take_partial(0)
    answers = []
    for step in range(1, heads):
        a_send[step - 1] = respond(step)
        copy = pltpu.make_async_remote_copy(
            src_ref=a_send.at[step - 1],
            dst_ref=a_recv.at[heads - step],
            send_sem=asend.at[step - 1],
            recv_sem=arecv.at[heads - step - 1],
            device_id=head_peer(step),
            device_id_type=MESH,
        )
        copy.start()
        answers.append(copy)
    a_recv[0] = respond(0)
    for copy in answers:
        copy.wait_recv()
    for h in range(heads):
        slot = lax.rem(h - me + heads, heads)
        out_ref[:, h * hd : (h + 1) * hd] = a_recv[slot]

    for copy in answers + every:
        copy.wait_send()

    def sent(k, carry):
        for step in range(1, heads):
            tok_send(step, k).wait_send()
        return carry

    lax.fori_loop(first, nk, sent, 0)


def body(mesh, tokens, w_qkv, scale_exp, gate_mask, rate, fast_gate, fast_up, fast_down):
    heads, seq = mesh.shape["head"], mesh.shape["seq"]
    t, d = tokens.shape
    hd, hid = fast_gate.shape[1:]
    blocks = scale_exp.shape[1]
    sb = d // blocks
    kc = sb * (4 if blocks % 4 == 0 else 1)
    nk = d // kc
    factors, padded, chunks = plan(seq, 3 * hd)
    span = padded // chunks
    parts = []
    size = span
    for f in factors:
        size //= f
        parts.append(size)
    dma = pltpu.SemaphoreType.DMA
    vmem = pl.BlockSpec(memory_space=pltpu.VMEM)
    smem = pl.BlockSpec(memory_space=pltpu.SMEM)
    hbm = pl.BlockSpec(memory_space=pl.ANY)
    most = max(factors) - 1
    depth = shared_depth(heads, seq, d, hd, kc)
    width = max(depth // (seq // 2), 128)
    f1, f2 = factors[1:]
    return pl.pallas_call(
        functools.partial(kernel, (heads, seq, kc, nk, sb, factors, padded, chunks, depth)),
        out_shape=jax.ShapeDtypeStruct((t, heads * hd), BF16),
        in_specs=[hbm, hbm, smem, vmem, smem, vmem, vmem, vmem],
        out_specs=vmem,
        scratch_shapes=[
            pltpu.VMEM((heads, t, d), BF16),
            pltpu.VMEM((3, hd, d), BF16),
            pltpu.VMEM((3, heads, t, hd), F32),
            pltpu.VMEM((3, hd, hid), F32),
            pltpu.VMEM((padded, hid), BF16),
            pltpu.VMEM((padded, hid), BF16),
            pltpu.VMEM((chunks, factors[0] - 1, parts[0], hid), BF16),
            pltpu.VMEM((chunks, factors[1] - 1, parts[1], hid), BF16),
            pltpu.VMEM((chunks, factors[2] - 1, parts[2], hid), BF16),
            pltpu.VMEM((3, hd, hid), BF16),
            pltpu.VMEM((heads - 1, t, hd), BF16),
            pltpu.VMEM((heads, t, hd), BF16),
            pltpu.VMEM((heads * t, 128), F32),
            pltpu.VMEM((3, hd // 2, width), BF16),
            pltpu.VMEM((3, hd, max(depth, 128)), BF16),
            pltpu.VMEM((t, hd), F32),
            pltpu.VMEM((3, t, hd), BF16),
            pltpu.VMEM((3, t, hd), BF16),
            dma((nk,)),
            dma((nk,)),
            dma((heads - 1, nk)),
            dma((heads - 1, nk)),
            dma((chunks, 3, most)),
            dma((chunks, 3, most)),
            dma((chunks, 3, most)),
            dma((chunks, 3, most)),
            dma((heads - 1,)),
            dma((heads - 1,)),
            dma((1,)),
            dma((3,)),
            dma((3,)),
            dma((3, f2 - 1)),
            dma((3, f2 - 1)),
            dma((3, f2, f1 - 1)),
            dma((3, f2, f1 - 1)),
            dma((3, f2, f1)),
            dma((3, f2, f1)),
            dma((3,)),
            dma((3,)),
        ],
        compiler_params=pltpu.CompilerParams(
            collective_id=0, has_side_effects=True, vmem_limit_bytes=60 * 1024 * 1024
        ),
    )(
        tokens, w_qkv.swapaxes(1, 2), scale_exp.swapaxes(1, 2), gate_mask.swapaxes(0, 1), rate,
        fast_gate, fast_up, fast_down,
    )


def solution(mesh):
    in_specs = (
        P(("seq", "head"), None),
        P(None, None, "head"),
        P(None, None, "head"),
        P("seq", "head"),
        P("head"),
        P("head", None, None),
        P("head", None, None),
        P("head", None, None),
    )
    out_specs = P(("seq", "head"), None)
    return jax.shard_map(
        functools.partial(body, mesh), mesh=mesh, in_specs=in_specs, out_specs=out_specs, check_vma=False
    )
```
